32 devices in a mesh: head: 4 (over x, core), ctx: 8 (over z, y).
Axes of the slice: x: 2, y: 2, z: 4, core: 2. Of those that a mesh axis runs over, the one named last changes fastest.
Arguments:
- queries: bfloat16 [4096, 512], P(('ctx', 'head')), may hold values from -24 to 24
- key_vectors: bfloat16 [4096, 512], P(('ctx', 'head')), may hold values from -24 to 24
- value_vectors: bfloat16 [4096, 512], P(('ctx', 'head')), may hold values from -24 to 24
- window: int32 [4], P('head'), may hold values from 48 to 384, as said below
- block_order: int32 [32], replicated, may hold values from 0 to 31, as said below
Outputs:
- grad_queries: float32 [4096, 512], P('ctx', 'head')
- grad_keys: float32 [4096, 512], P('ctx', 'head')
- grad_values: float32 [4096, 512], P('ctx', 'head')
The draws below stay inside these ranges and needn't reach their ends.
Inputs may be any that keep to these rules, and one draw needn't show every extreme that they name: `window`: some head has the reach 384 exactly. `block_order`: a permutation of 0 to 31 that maps each aligned group of 4 entries onto itself: entry g and its value lie in the same group.
All inputs are finite; a program needn't handle non-finite values.
Results may differ from the reference program's by a relative error of at most 0.039.
Values may be sent and summed in bfloat16 or wider, within the bound.
A program may use at most 64 MiB of HBM per device.

```python
import jax
import jax.numpy as jnp
from jax import lax

DH = 128
TOK_CTX = 512
BLK = 128
RMAX = 384
HEADS = 4
TOKENS = 4096


def paired_vectors(key):
    base_key = jax.random.fold_in(key, 17)
    subkeys = jax.random.split(base_key, 2)
    full_shape = (TOKENS, HEADS * DH)
    query_draw = jnp.clip(jax.random.normal(subkeys[0], full_shape, jnp.float32), -6.0, 6.0)
    key_draw = jnp.clip(jax.random.normal(subkeys[1], full_shape, jnp.float32), -6.0, 6.0)
    return (query_draw, key_draw)


def draw_queries(key, part):
    return paired_vectors(key)[0].astype(jnp.bfloat16)


def draw_key_vectors(key, part):
    return paired_vectors(key)[1].astype(jnp.bfloat16)


def draw_window(key, part):
    subkeys = jax.random.split(jax.random.fold_in(key, 23), 2)
    reaches = jax.random.randint(subkeys[0], (HEADS,), RMAX // 8, RMAX + 1)
    widest = jax.random.randint(subkeys[1], (), 0, HEADS)
    return jnp.where(jnp.arange(HEADS) == widest, RMAX, reaches).astype(jnp.int32)


def draw_block_order(key, part):
    blocks_shard = TOK_CTX // BLK
    groups = TOKENS // TOK_CTX
    ranking = jax.random.randint(jax.random.fold_in(key, 29), (groups, blocks_shard), 0, 1048576)
    distinct = ranking * blocks_shard + jnp.arange(blocks_shard, dtype=jnp.int32)[None, :]
    ordering = jnp.argsort(distinct, axis=1, stable=True).astype(jnp.int32)
    return (ordering + jnp.arange(groups, dtype=jnp.int32)[:, None] * blocks_shard).reshape(groups * blocks_shard).astype(jnp.int32)


def steps_of(rng, shape, cuts, least, largest):
    def one(dim, shards_of):
        draws = jax.random.uniform(jax.random.fold_in(jax.random.fold_in(rng, 6), dim), (shards_of,), jnp.float32, least / len(cuts), largest / len(cuts))
        return jnp.repeat(jnp.exp(draws), shape[dim] // shards_of).reshape((-1,) + (1,) * (len(shape) - dim - 1))

    level = one(*cuts[0])
    for cut in cuts[1:]:
        level = level * one(*cut)
    return level


def scatter_about(own_key, extent, width, limit, cuts=(), held_as=jnp.bfloat16):
    values = jax.random.normal(own_key, extent, jnp.float32) * width
    if len(cuts) > 0:
        values = steps_of(own_key, extent, cuts, -0.22, 0.18) * values
    return jnp.clip(values, min=-limit, max=limit).astype(held_as)


def setup_inputs(seed: int = 0) -> dict:
    keys = jax.random.split(jax.random.key(seed), 6)
    queries = draw_queries(jax.random.fold_in(keys[5], 71), 0)
    key_vectors = draw_key_vectors(jax.random.fold_in(keys[5], 71), 0)
    value_vectors = scatter_about(keys[2], (TOKENS, HEADS * DH), 4.0, 24.0, ((0, 32),))
    window = draw_window(jax.random.fold_in(keys[5], 71), 0)
    block_order = draw_block_order(jax.random.fold_in(keys[5], 71), 0)
    return {"queries": queries, "key_vectors": key_vectors, "value_vectors": value_vectors, "window": window, "block_order": block_order}


def rounded(values):
    return lax.optimization_barrier(values.astype(jnp.bfloat16)).astype(jnp.float32)


def matmul(left, right):
    return jnp.dot(left, right, preferred_element_type=jnp.float32, precision=lax.Precision.HIGHEST)


def token_positions(block_order):
    inside = jnp.arange(TOKENS, dtype=jnp.int32) % BLK
    return jnp.repeat(block_order, BLK, total_repeat_length=TOKENS) * BLK + inside


def head_grads(query_head, key_head, value_head, reach_head, position):
    score_scale = DH ** -0.5
    shard_count = TOKENS // TOK_CTX
    key_padded = jnp.pad(key_head, ((TOK_CTX, TOK_CTX), (0, 0)))
    value_padded = jnp.pad(value_head, ((TOK_CTX, TOK_CTX), (0, 0)))
    position_padded = jnp.pad(position, TOK_CTX, constant_values=-4 * TOKENS)

    def shard_step(running, shard_number):
        key_total, value_total = running
        offset = (shard_number * TOK_CTX).astype(jnp.int32)
        query_block = lax.dynamic_slice_in_dim(query_head, offset, TOK_CTX, 0)
        query_place = lax.dynamic_slice_in_dim(position, offset, TOK_CTX, 0)
        teacher_scores = matmul(query_block, key_head.T) * score_scale
        teacher_top = jnp.max(teacher_scores, axis=1, keepdims=True)
        teacher_weights = jnp.exp(teacher_scores - teacher_top)
        teacher = matmul(rounded(teacher_weights), value_head) / jnp.sum(teacher_weights, axis=1, keepdims=True)
        key_near = lax.dynamic_slice_in_dim(key_padded, offset, 3 * TOK_CTX, 0)
        value_near = lax.dynamic_slice_in_dim(value_padded, offset, 3 * TOK_CTX, 0)
        place_near = lax.dynamic_slice_in_dim(position_padded, offset, 3 * TOK_CTX, 0)
        scores = matmul(query_block, key_near.T) * score_scale
        nearby = jnp.abs(query_place[:, None] - place_near[None, :]) <= reach_head
        student_top = jnp.max(jnp.where(nearby, scores, -jnp.inf), axis=1, keepdims=True)
        weights = jnp.where(nearby, jnp.exp(scores - student_top), 0.0)
        prob = weights / jnp.sum(weights, axis=1, keepdims=True)
        prob_b = rounded(prob)
        student = matmul(prob_b, value_near)
        mismatch = student - teacher
        mismatch_b = rounded(mismatch)
        row_delta = jnp.sum(mismatch * student, axis=1, keepdims=True)
        dprob = matmul(mismatch_b, value_near.T)
        dscore = rounded(prob * (dprob - row_delta))
        grad_query = matmul(dscore, key_near) * score_scale
        grad_key = matmul(dscore.T, query_block) * score_scale
        grad_value = matmul(prob_b.T, mismatch_b)
        key_total = lax.dynamic_update_slice_in_dim(key_total, lax.dynamic_slice_in_dim(key_total, offset, 3 * TOK_CTX, 0) + grad_key, offset, 0)
        value_total = lax.dynamic_update_slice_in_dim(value_total, lax.dynamic_slice_in_dim(value_total, offset, 3 * TOK_CTX, 0) + grad_value, offset, 0)
        return (key_total, value_total), grad_query

    empty = jnp.zeros((TOKENS + 2 * TOK_CTX, DH), jnp.float32)
    totals, grad_query = lax.scan(shard_step, (empty, empty), jnp.arange(shard_count, dtype=jnp.int32))
    key_total, value_total = totals
    return grad_query.reshape(TOKENS, DH), key_total[TOK_CTX:TOK_CTX + TOKENS], value_total[TOK_CTX:TOK_CTX + TOKENS]


def reference(queries, key_vectors, value_vectors, window, block_order):
    position = token_positions(block_order)

    def by_head(values):
        return values.astype(jnp.float32).reshape(TOKENS, HEADS, DH).transpose(1, 0, 2)

    def one_head(inputs):
        query_head, key_head, value_head, reach_head = inputs
        return head_grads(query_head, key_head, value_head, reach_head, position)

    grad_query, grad_key, grad_value = lax.map(one_head, (by_head(queries), by_head(key_vectors), by_head(value_vectors), window))

    def joined(values):
        return values.transpose(1, 0, 2).reshape(TOKENS, HEADS * DH)

    return joined(grad_query), joined(grad_key), joined(grad_value)
```

```python
import functools

import jax
import jax.numpy as jnp
from jax import lax
from jax.experimental import pallas as pl
from jax.experimental.pallas import tpu as pltpu
from jax.sharding import PartitionSpec as P

DH = 128
BLK = 128
RMAX = 384
HALO = RMAX // BLK
LOG2E = 1.4426950408889634
MESH = pl.DeviceIdType.MESH
NEG = -1e30


def dot_nt(a, b):
    return lax.dot_general(a, b, (((1,), (1,)), ((), ())), preferred_element_type=jnp.float32)


def dot_nn(a, b):
    return lax.dot_general(a, b, (((1,), (0,)), ((), ())), preferred_element_type=jnp.float32)


def dot_tn(a, b):
    return lax.dot_general(a, b, (((0,), (0,)), ((), ())), preferred_element_type=jnp.float32)


def grid_of(n):
    ny = 1
    while ny * ny * 8 <= n and n % (ny * 2) == 0:
        ny *= 2
    return n // ny, ny


def place_of(index, n):
    nz, ny = grid_of(n)
    z, y = index // ny, index % ny
    odd = y % 2
    return y * nz + z * (1 - odd) + (nz - 1 - z) * odd


def index_at(place, n):
    nz, ny = grid_of(n)
    y, r = place // nz, place % nz
    odd = y % 2
    z = r * (1 - odd) + (nz - 1 - r) * odd
    return z * ny + y


def kernel(
    n, g,
    window_ref, order_ref, q_ref, k_ref, v_ref,
    gq_s, gk_s, gv_s,
    qx, kv, qs, kpos, vpos, top_s, sum_s, acc_s, reach_s,
    a_send, a_recv, q_send, q_recv, r_send, r_recv, w_sem,
):
    c = lax.axis_index("ctx")
    h = lax.axis_index("head")
    part = q_ref.shape[0]
    rows = part * g
    nb = rows // BLK
    pieces = min(g, 4)
    per = g // pieces
    prow = rows // pieces
    half = n // 2
    nq = nb + 2 * HALO
    nk = nb + 4 * HALO
    scale = DH ** -0.5
    scale2 = scale * LOG2E
    assert nb >= HALO
    place = place_of(c, n)
    right = index_at((place + 1) % n, n)
    left = index_at((place + n - 1) % n, n)
    ways = (right, left)

    barrier = pltpu.get_barrier_semaphore()
    for d in range(1, g):
        pl.semaphore_signal(barrier, inc=1, device_id={"head": (h + d) % g}, device_id_type=MESH)
    for way in ways:
        pl.semaphore_signal(barrier, inc=1, device_id={"ctx": way}, device_id_type=MESH)

    @pl.when(c > 0)
    def _():
        pl.semaphore_signal(barrier, inc=1, device_id={"ctx": c - 1}, device_id_type=MESH)

    @pl.when(c < n - 1)
    def _():
        pl.semaphore_signal(barrier, inc=1, device_id={"ctx": c + 1}, device_id_type=MESH)

    reach_copy = pltpu.make_async_copy(window_ref, reach_s, w_sem.at[0])
    reach_copy.start()
    pl.semaphore_wait(barrier, g + 1 + jnp.minimum(c, 1) + jnp.minimum(n - 1 - c, 1))

    mine = pl.ds(pl.multiple_of(h * part, part), part)

    def spread(d, which):
        peer = (h + d) % g
        cols = pl.ds(pl.multiple_of(peer * DH, DH), DH)
        src = (k_ref, v_ref, q_ref)[which].at[:, cols]
        dst = qx.at[mine] if which == 2 else kv.at[c, which, mine]
        if d == 0:
            return pltpu.make_async_copy(src, dst, a_recv.at[which, 0])
        return pltpu.make_async_remote_copy(
            src_ref=src, dst_ref=dst, send_sem=a_send.at[which, d], recv_sem=a_recv.at[which, d],
            device_id={"head": peer}, device_id_type=MESH,
        )

    for d in range(g):
        spread(d, 0).start()
        spread(d, 1).start()
    for d in range(g):
        spread(d, 2).start()

    def arrived(d, which):
        if d == 0:
            spread(0, which).wait()
        else:
            spread(d, which).wait_recv()

    def piece_of(d):
        return (h // per + pieces - d) % pieces

    def hop(way, step, d):
        sign = 1 if way == 0 else n - 1
        owner = index_at((place + step * (n - sign)) % n, n)
        span = pl.ds(pl.multiple_of(piece_of(d) * prow, prow), prow)
        ref = kv.at[owner, :, span]
        return pltpu.make_async_remote_copy(
            src_ref=ref, dst_ref=ref, send_sem=r_send.at[way, step, d], recv_sem=r_recv.at[way, step, d],
            device_id={"ctx": ways[way]}, device_id_type=MESH,
        )

    def landed(way, step, d):
        hop(way, step, d).wait_recv()

    if per == 1:
        for d in range(pieces):
            arrived(d, 0)
            arrived(d, 1)
            for way in range(2):
                hop(way, 0, d).start()
    else:
        for d in range(g):
            arrived(d, 0)
            arrived(d, 1)
        for d in range(pieces):
            for way in range(2):
                hop(way, 0, d).start()
    for d in range(g):
        arrived(d, 2)

    def picked(blocks, group, p):
        found = blocks(0)
        for i in range(1, nb):
            found = jnp.where(order_ref[group * nb + i] == group * nb + p, blocks(i), found)
        return found

    edge = HALO * BLK
    for p in range(nb):
        qs[pl.ds(edge + p * BLK, BLK), :] = picked(lambda i: qx[pl.ds(i * BLK, BLK), :], c, p)

    top_s[...] = jnp.full(top_s.shape, NEG, jnp.float32)
    sum_s[...] = jnp.zeros(sum_s.shape, jnp.float32)
    acc_s[...] = jnp.zeros(acc_s.shape, jnp.float32)

    def beside(up):
        return pltpu.make_async_remote_copy(
            src_ref=qs.at[pl.ds(rows if up else edge, edge)],
            dst_ref=qs.at[pl.ds(0 if up else edge + rows, edge)],
            send_sem=q_send.at[1 if up else 0], recv_sem=q_recv.at[1 if up else 0],
            device_id={"ctx": (c + 1) if up else (c - 1)}, device_id_type=MESH,
        )

    @pl.when(c > 0)
    def _():
        beside(False).start()

    @pl.when(c == 0)
    def _():
        qs[pl.ds(0, edge), :] = jnp.zeros((edge, DH), jnp.bfloat16)

    @pl.when(c < n - 1)
    def _():
        beside(True).start()

    @pl.when(c == n - 1)
    def _():
        qs[pl.ds(edge + rows, edge), :] = jnp.zeros((edge, DH), jnp.bfloat16)

    def sends_at(way, d, step_last):
        return (not step_last) or ((d < pieces // 2) == (way == 0))

    def forward(step, step_last, d):
        for way in range(2):
            landed(way, step - 1, d)
            if sends_at(way, d, step_last):
                hop(way, step, d).start()

    for d in range(pieces):
        forward(1, half == 2, d)

    @pl.when(c > 0)
    def _():
        beside(True).wait_recv()

    @pl.when(c < n - 1)
    def _():
        beside(False).wait_recv()

    groups = {}
    for off in range(-2, 3):
        groups[off] = jnp.clip(c + off, 0, n - 1)

    qrow = nq * BLK // pieces

    def fold(u, owners, size=qrow):
        span = pl.ds(u * size, size)
        q = qs[span, :]
        scores = [dot_nt(q, kv[o, 0]) * scale2 for o in owners]
        top_old = top_s[span, :]
        highest = scores[0]
        for s in scores[1:]:
            highest = jnp.maximum(highest, s)
        top = jnp.maximum(top_old, jnp.max(highest, axis=1, keepdims=True))
        shrink = jnp.exp2(top_old - top)
        total = sum_s[span, :] * shrink
        acc = acc_s[span, :] * shrink
        for s, o in zip(scores, owners):
            e = jnp.exp2(s - top[:, :1])
            for i in range(rows // 128):
                total = total + e[:, i * 128 : (i + 1) * 128]
            acc = acc + dot_nn(e.astype(jnp.bfloat16), kv[o, 1])
        top_s[span, :] = top
        sum_s[span, :] = total
        acc_s[span, :] = acc

    def pair_at(step):
        return [index_at((place + n - step) % n, n), index_at((place + step) % n, n)]

    for u in range(pieces):
        fold(u, [c])

    def middle(step, carry):
        for d in range(pieces):
            forward(step, False, d)
            fold(d, pair_at(step - 1))
        return carry

    if half > 2:
        lax.fori_loop(2, half - 1, middle, 0)
        for d in range(pieces):
            forward(half - 1, True, d)
            fold(d, pair_at(half - 2))
    for d in range(pieces):
        fold(d, pair_at(half - 1))
    for d in range(pieces):
        for way in range(2):
            if sends_at(way, d, True):
                landed(way, half - 1, d)
    reach_copy.wait()
    for k in range(nk):
        off, p = (k - 2 * HALO) // nb, (k - 2 * HALO) % nb
        group = groups[off]
        for which, to in ((0, kpos), (1, vpos)):
            to[pl.ds(k * BLK, BLK), :] = picked(
                lambda i: kv[group, which, pl.ds(i * BLK, BLK), :], group, p
            )

    reach = reach_s[0]
    unit = 2
    units = nq // unit
    wide = 2 * HALO + unit
    usize = unit * BLK
    last = [index_at((place + half) % n, n)]
    gk_s[...] = jnp.zeros(gk_s.shape, jnp.float32)
    gv_s[...] = jnp.zeros(gv_s.shape, jnp.float32)
    held = {}

    def student_of(u):
        m = u * unit
        keys = pl.ds(m * BLK, wide * BLK)
        s = dot_nt(qs[pl.ds(m * BLK, usize), :], kpos[keys, :]) * scale2
        first = (c * nb + m - 2 * HALO) * BLK
        i = lax.broadcasted_iota(jnp.int32, (usize, 1), 0)
        j = lax.broadcasted_iota(jnp.int32, (usize, wide * BLK), 1)
        position = i + (first + HALO * BLK)
        i = i + HALO * BLK
        present = jnp.logical_and(position >= 0, position < n * rows)
        low = jnp.maximum(i - reach, -first)
        high = jnp.minimum(i + reach, n * rows - 1 - first)
        s = jnp.where(jnp.logical_and(j >= low, j <= high), s, NEG)
        top = jnp.max(s, axis=1, keepdims=True)
        e = jnp.exp2(s - top)
        inverse = jnp.where(present, 1.0 / jnp.sum(e, axis=1, keepdims=True), 0.0)
        prob = e * inverse
        prob_b = prob.astype(jnp.bfloat16)
        held[u] = (prob, prob_b, dot_nn(prob_b, vpos[keys, :]))

    def back_of(u):
        prob, prob_b, student = held.pop(u)
        m = u * unit
        span = pl.ds(m * BLK, usize)
        teacher = acc_s[span, :] * (1.0 / jnp.sum(sum_s[span, :], axis=1, keepdims=True))
        mismatch = student - teacher
        mismatch_b = mismatch.astype(jnp.bfloat16)
        delta = jnp.sum(mismatch * student, axis=1, keepdims=True)
        k0 = max(m, 2 * HALO)
        k1 = min(m + wide, 2 * HALO + nb)
        a0, a1 = (k0 - m) * BLK, (k1 - m) * BLK
        own = m + unit > HALO and m < HALO + nb
        if own:
            keys = pl.ds(m * BLK, wide * BLK)
            dprob = dot_nt(mismatch_b, vpos[keys, :])
            dscore = (prob * (dprob - delta)).astype(jnp.bfloat16)
            r0 = max(HALO - m, 0) * BLK
            r1 = min(HALO + nb - m, unit) * BLK
            gq_s[pl.ds((m - HALO) * BLK + r0, r1 - r0), :] = dot_nn(dscore[r0:r1], kpos[keys, :])
            dscore = dscore[:, a0:a1]
        else:
            dprob = dot_nt(mismatch_b, vpos[pl.ds(k0 * BLK, a1 - a0), :])
            dscore = (prob[:, a0:a1] * (dprob - delta)).astype(jnp.bfloat16)
        out = pl.ds((k0 - 2 * HALO) * BLK, a1 - a0)
        gk_s[out, :] += dot_tn(dscore, qs[span, :])
        gv_s[out, :] += dot_tn(prob_b[:, a0:a1], mismatch_b)

    for u in range(units + 1):
        if u < units:
            fold(u, last, usize)
            student_of(u)
        if u > 0:
            back_of(u - 1)

    for which in range(3):
        for d in range(1, g):
            spread(d, which).wait_send()

    @pl.when(c > 0)
    def _():
        beside(False).wait_send()

    @pl.when(c < n - 1)
    def _():
        beside(True).wait_send()

    def drain(step, carry):
        for d in range(pieces):
            for way in range(2):
                hop(way, step, d).wait_send()
        return carry

    lax.fori_loop(0, half - 1, drain, 0)
    for d in range(pieces):
        for way in range(2):
            if sends_at(way, d, True):
                hop(way, half - 1, d).wait_send()


def finish(order_ref, gq_s, gk_s, gv_s, gq_ref, gk_ref, gv_ref):
    nb = gq_ref.shape[0] // BLK
    c = lax.axis_index("ctx")
    scale = DH ** -0.5
    for b in range(nb):
        at = pl.ds(pl.multiple_of((order_ref[c * nb + b] - c * nb) * BLK, BLK), BLK)
        to = pl.ds(b * BLK, BLK)
        gq_ref[to, :] = gq_s[at, :] * scale
        gk_ref[to, :] = gk_s[at, :] * scale
        gv_ref[to, :] = gv_s[at, :]


def solution(mesh):
    n, g = mesh.shape["ctx"], mesh.shape["head"]

    def body(queries, key_vectors, value_vectors, window, block_order):
        part, width = queries.shape
        rows = part * g
        assert width == g * DH and rows % BLK == 0 and n >= 4 and n % 2 == 0
        nb = rows // BLK
        pieces = min(g, 4)
        half = n // 2
        tall_q = (nb + 2 * HALO) * BLK
        tall_k = (nb + 4 * HALO) * BLK
        out = jax.ShapeDtypeStruct((rows, DH), jnp.float32)
        vmem = pl.BlockSpec(memory_space=pltpu.VMEM)
        smem = pl.BlockSpec(memory_space=pltpu.SMEM)
        hbm = pl.BlockSpec(memory_space=pltpu.HBM)
        grads = pl.pallas_call(
            functools.partial(kernel, n, g),
            out_shape=(out, out, out),
            in_specs=[hbm, smem, hbm, hbm, hbm],
            out_specs=(vmem, vmem, vmem),
            scratch_shapes=[
                pltpu.VMEM((rows, DH), jnp.bfloat16),
                pltpu.VMEM((n, 2, rows, DH), jnp.bfloat16),
                pltpu.VMEM((tall_q, DH), jnp.bfloat16),
                pltpu.VMEM((tall_k, DH), jnp.bfloat16),
                pltpu.VMEM((tall_k, DH), jnp.bfloat16),
                pltpu.VMEM((tall_q, DH), jnp.float32),
                pltpu.VMEM((tall_q, DH), jnp.float32),
                pltpu.VMEM((tall_q, DH), jnp.float32),
                pltpu.SMEM((1,), jnp.int32),
                pltpu.SemaphoreType.DMA((3, g)),
                pltpu.SemaphoreType.DMA((3, g)),
                pltpu.SemaphoreType.DMA((2,)),
                pltpu.SemaphoreType.DMA((2,)),
                pltpu.SemaphoreType.DMA((2, half, pieces)),
                pltpu.SemaphoreType.DMA((2, half, pieces)),
                pltpu.SemaphoreType.DMA((1,)),
            ],
            compiler_params=pltpu.CompilerParams(collective_id=0, has_side_effects=True),
        )(window, block_order, queries, key_vectors, value_vectors)
        return pl.pallas_call(
            finish,
            out_shape=(out, out, out),
            in_specs=[smem, vmem, vmem, vmem],
            out_specs=(vmem, vmem, vmem),
        )(block_order, *grads)

    in_specs = (
        P(("ctx", "head"), None),
        P(("ctx", "head"), None),
        P(("ctx", "head"), None),
        P("head"),
        P(),
    )
    out_specs = (P("ctx", "head"), P("ctx", "head"), P("ctx", "head"))
    return jax.shard_map(body, mesh=mesh, in_specs=in_specs, out_specs=out_specs, check_vma=False)
```
